32 devices in a mesh: rep: 16 (over z, y, core), grp: 2 (over x).
Axes of the slice: x: 2, y: 2, z: 4, core: 2. Of those that a mesh axis runs over, the one named last changes fastest.
Arguments:
- tokens: bfloat16 [16, 256, 1088], P('rep', 'grp'), may hold values from -6 to 6
- cotangent: bfloat16 [16, 256, 1088], P('rep', 'grp'), may hold values from -6 to 6
- positions: int32 [16, 256], P('rep'), may hold values from 0 to 255, as said below
- ln1_gain: bfloat16 [1088], P('grp'), may hold values from 0.099609375 to 1.8984375
- ln1_bias: bfloat16 [1088], P('grp'), may hold values from -3 to 3
- w_qkv: bfloat16 [1088, 3264], P('grp'), may hold values from -0.1875 to 0.1875
- qv_bias: bfloat16 [2176], P('grp'), may hold values from -3 to 3
- w_out: bfloat16 [1088, 1088], P('grp'), may hold values from -2 to 2
- out_bias: bfloat16 [1088], P('grp'), may hold values from -3 to 3
- ln2_gain: bfloat16 [1088], P('grp'), may hold values from 0.099609375 to 1.8984375
- ln2_bias: bfloat16 [1088], P('grp'), may hold values from -3 to 3
- w_up: bfloat16 [1088, 4352], P('grp'), may hold values from -0.1875 to 0.1875
- up_bias: bfloat16 [4352], P('grp'), may hold values from -3 to 3
- w_down: bfloat16 [4352, 1088], P('grp'), may hold values from -0.09375 to 0.09375
- down_bias: bfloat16 [1088], P('grp'), may hold values from -3 to 3
Outputs:
- output: float32 [16, 256, 1088], P('rep', 'grp')
- grad_tokens: float32 [16, 256, 1088], P('rep', 'grp')
- grad_ln1_gain: float32 [1088], P('grp')
- grad_ln1_bias: float32 [1088], P('grp')
- grad_w_qkv: float32 [1088, 3264], P('grp')
- grad_qv_bias: float32 [2176], P('grp')
- grad_w_out: float32 [1088, 1088], P('grp')
- grad_out_bias: float32 [1088], P('grp')
- grad_ln2_gain: float32 [1088], P('grp')
- grad_ln2_bias: float32 [1088], P('grp')
- grad_w_up: float32 [1088, 4352], P('grp')
- grad_up_bias: float32 [4352], P('grp')
- grad_w_down: float32 [4352, 1088], P('grp')
- grad_down_bias: float32 [1088], P('grp')
The draws below stay inside these ranges and needn't reach their ends.
Inputs may be any that keep to these rules, and one draw needn't show every extreme that they name: Each row is a permutation of 0 to 255 made of runs of 64 consecutive rising positions; each run fills an aligned run of 64 slots and starts at a multiple of 64; each sequence's order of runs is drawn independently of the others.
All inputs are finite; a program needn't handle non-finite values.
Results may differ from the reference program's by a relative error of at most 0.012.
Values may be sent and summed in bfloat16 or wider, within the bound.
No kernel may reach another device: no remote copies, remote signals or barrier semaphores. Data moves between devices by JAX's collectives and lax.ppermute only.
A program may use at most 192 MiB of HBM per device.

```python
import math
import jax
import jax.numpy as jnp
from jax import lax

HEADS = 17
HEAD = 64
D = 1088
FF = 4352
BLOCK = 128
LEN = 256
NSEQ = 16


def draw_positions(key, part):
    half_run = BLOCK // 2
    count_runs = LEN // half_run
    seq_keys = jax.random.split(jax.random.fold_in(key, 7), NSEQ)
    orders = jax.vmap(lambda one_key: jax.random.permutation(one_key, count_runs))(seq_keys)
    placed = orders[:, :, None] * half_run + jnp.arange(half_run, dtype=jnp.int32)[None, None, :]
    return placed.reshape(NSEQ, LEN).astype(jnp.int32)


def steps_of(own_key, dims, shards, least, top_value):
    loudness = 1.0
    for axis_at, shards_of in shards:
        heights = jax.random.uniform(jax.random.fold_in(jax.random.fold_in(own_key, 6), axis_at), (shards_of,), jnp.float32, least / len(shards), top_value / len(shards))
        loudness = loudness * jnp.repeat(jnp.exp(heights), dims[axis_at] // shards_of).reshape((-1,) + (1,) * (len(dims) - 1 - axis_at))
    return loudness


def bell_draw(own_key, shape, width, reach, shards=(), kind=jnp.bfloat16):
    array = width * jax.random.normal(own_key, shape, jnp.float32)
    if shards:
        array = array * steps_of(own_key, shape, shards, -0.22, 0.18)
    return jnp.clip(array, -reach, reach).astype(kind)


def setup_inputs(seed: int = 0) -> dict:
    arg_keys = jax.random.split(jax.random.key(seed), 16)
    return {
        "tokens": bell_draw(arg_keys[0], (NSEQ, LEN, D), 1.0, 6.0, ((0, 16), (1, 2))),
        "cotangent": bell_draw(arg_keys[1], (NSEQ, LEN, D), 1.0, 6.0, ((0, 16), (1, 2))),
        "positions": draw_positions(jax.random.fold_in(arg_keys[15], 71), 0),
        "ln1_gain": jnp.clip(1.0 + 0.18 * jax.random.normal(arg_keys[3], (D,), jnp.float32), 0.099609375, 1.8984375).astype(jnp.bfloat16),
        "ln1_bias": bell_draw(arg_keys[4], (D,), 0.5, 3.0, ((0, 2),)),
        "w_qkv": bell_draw(arg_keys[5], (D, 3 * D), D ** -0.5, 0.1875, ((0, 2),)),
        "qv_bias": bell_draw(arg_keys[6], (2 * D,), 0.5, 3.0, ((0, 2),)),
        "w_out": bell_draw(arg_keys[7], (D, D), (max(2 * D // LEN, 1)) ** -0.5, 2.0, ((0, 2),)),
        "out_bias": bell_draw(arg_keys[8], (D,), 0.5, 3.0, ((0, 2),)),
        "ln2_gain": jnp.clip(1.0 + 0.18 * jax.random.normal(arg_keys[9], (D,), jnp.float32), 0.099609375, 1.8984375).astype(jnp.bfloat16),
        "ln2_bias": bell_draw(arg_keys[10], (D,), 0.5, 3.0, ((0, 2),)),
        "w_up": bell_draw(arg_keys[11], (D, FF), D ** -0.5, 0.1875, ((0, 2),)),
        "up_bias": bell_draw(arg_keys[12], (FF,), 0.5, 3.0, ((0, 2),)),
        "w_down": bell_draw(arg_keys[13], (FF, D), FF ** -0.5, 0.09375, ((0, 2),)),
        "down_bias": bell_draw(arg_keys[14], (D,), 0.5, 3.0, ((0, 2),)),
    }


EPS = 1e-05
GELU_C = 0.7978845608028654

def gelu_value(hidden):
    return 0.5 * hidden * (1.0 + jnp.tanh(GELU_C * (hidden + 0.044715 * hidden * hidden * hidden)))

def gelu_slope(hidden):
    inner = jnp.tanh(GELU_C * (hidden + 0.044715 * hidden * hidden * hidden))
    return 0.5 * (1.0 + inner) + 0.5 * hidden * (1.0 - inner * inner) * GELU_C * (1.0 + 3.0 * 0.044715 * hidden * hidden)

def norm_apply(values):
    centred = values - lax.optimization_barrier(jnp.mean(values, -1, keepdims=True))
    inv_std = lax.rsqrt(lax.optimization_barrier(jnp.mean(centred * centred, -1, keepdims=True)) + EPS)
    return (centred * inv_std, inv_std)

def norm_back(grad_norm, normed, inv_std):
    return inv_std * (grad_norm - lax.optimization_barrier(jnp.mean(grad_norm, -1, keepdims=True)) - normed * lax.optimization_barrier(jnp.mean(grad_norm * normed, -1, keepdims=True)))

def reference(tokens, cotangent, positions, ln1_gain, ln1_bias, w_qkv, qv_bias, w_out, out_bias, ln2_gain, ln2_bias, w_up, up_bias, w_down, down_bias):
    model = D
    heads = HEADS
    scale_qk = 1.0 / math.sqrt(HEAD)
    f32 = jnp.float32
    bf16 = jnp.bfloat16
    gain1 = ln1_gain.astype(f32)
    gain2 = ln2_gain.astype(f32)

    def one_sequence(carry, inputs):
        seq_tokens, seq_cot, seq_pos = inputs
        length = seq_tokens.shape[0]
        allowed = seq_pos[None, :] <= seq_pos[:, None]
        xfloat = seq_tokens.astype(f32)
        normed1, inv1 = norm_apply(xfloat)
        act1 = (normed1 * gain1 + ln1_bias.astype(f32)).astype(bf16)
        proj = jnp.dot(act1, w_qkv, preferred_element_type=f32)
        qv_f = qv_bias.astype(f32)
        query = (proj[:, :model] + qv_f[:model]).astype(bf16)
        keys = proj[:, model:2 * model].astype(bf16)
        values = (proj[:, 2 * model:] + qv_f[model:]).astype(bf16)
        query_h = query.reshape(length, heads, HEAD).astype(f32)
        keys_h = keys.reshape(length, heads, HEAD).astype(f32)
        values_h = values.reshape(length, heads, HEAD).astype(f32)
        scores = jnp.einsum('qhd,khd->hqk', query_h, keys_h) * scale_qk
        scores = jnp.where(allowed[None], scores, -jnp.inf)
        peak = lax.optimization_barrier(jnp.max(scores, -1, keepdims=True))
        log_total = peak + jnp.log(lax.optimization_barrier(jnp.sum(jnp.exp(scores - peak), -1, keepdims=True)))
        probs = jnp.exp(scores - log_total)
        probs_b = probs.astype(bf16)
        attended = jnp.einsum('hqk,khd->qhd', probs_b.astype(f32), values_h).reshape(length, model).astype(bf16)
        middle = xfloat + jnp.dot(attended, w_out, preferred_element_type=f32) + out_bias.astype(f32)
        normed2, inv2 = norm_apply(middle)
        act2 = (normed2 * gain2 + ln2_bias.astype(f32)).astype(bf16)
        hidden = jnp.dot(act2, w_up, preferred_element_type=f32) + up_bias.astype(f32)
        activ = gelu_value(hidden).astype(bf16)
        output = middle + jnp.dot(activ, w_down, preferred_element_type=f32) + down_bias.astype(f32)
        grad_f = seq_cot.astype(f32)
        g_down = jnp.dot(activ.T, seq_cot, preferred_element_type=f32)
        g_dbias = lax.optimization_barrier(jnp.sum(grad_f, 0))
        grad_act = jnp.dot(seq_cot, w_down.T, preferred_element_type=f32)
        grad_hidden = (grad_act * gelu_slope(hidden)).astype(bf16)
        g_up = jnp.dot(act2.T, grad_hidden, preferred_element_type=f32)
        g_ubias = lax.optimization_barrier(jnp.sum(grad_hidden.astype(f32), 0))
        grad_norm2 = jnp.dot(grad_hidden, w_up.T, preferred_element_type=f32)
        g_gain2 = lax.optimization_barrier(jnp.sum(grad_norm2 * normed2, 0))
        g_bias2 = lax.optimization_barrier(jnp.sum(grad_norm2, 0))
        grad_middle = grad_f + norm_back(grad_norm2 * gain2, normed2, inv2)
        grad_mid_b = grad_middle.astype(bf16)
        g_out = jnp.dot(attended.T, grad_mid_b, preferred_element_type=f32)
        g_obias = lax.optimization_barrier(jnp.sum(grad_middle, 0))
        grad_att = jnp.dot(grad_mid_b, w_out.T, preferred_element_type=f32).astype(bf16)
        grad_att_h = grad_att.reshape(length, heads, HEAD).astype(f32)
        attended_h = attended.reshape(length, heads, HEAD).astype(f32)
        again = jnp.where(allowed[None], jnp.einsum('qhd,khd->hqk', query_h, keys_h) * scale_qk, -jnp.inf)
        probs_again = jnp.exp(again - log_total)
        grad_probs = jnp.einsum('qhd,khd->hqk', grad_att_h, values_h)
        delta = jnp.einsum('qhd,qhd->hq', grad_att_h, attended_h)[..., None]
        grad_scores = (probs_again * (grad_probs - delta) * scale_qk).astype(bf16).astype(f32)
        grad_query = jnp.einsum('hqk,khd->qhd', grad_scores, keys_h).reshape(length, model)
        grad_keys = jnp.einsum('hqk,qhd->khd', grad_scores, query_h).reshape(length, model)
        grad_values = jnp.einsum('hqk,qhd->khd', probs_b.astype(f32), grad_att_h).reshape(length, model)
        grad_proj = jnp.concatenate([grad_query, grad_keys, grad_values], 1).astype(bf16)
        g_qkv = jnp.dot(act1.T, grad_proj, preferred_element_type=f32)
        g_qv = jnp.concatenate([lax.optimization_barrier(jnp.sum(grad_proj[:, :model].astype(f32), 0)), lax.optimization_barrier(jnp.sum(grad_proj[:, 2 * model:].astype(f32), 0))])
        grad_norm1 = jnp.dot(grad_proj, w_qkv.T, preferred_element_type=f32)
        g_gain1 = lax.optimization_barrier(jnp.sum(grad_norm1 * normed1, 0))
        g_bias1 = lax.optimization_barrier(jnp.sum(grad_norm1, 0))
        grad_inputs = grad_middle + norm_back(grad_norm1 * gain1, normed1, inv1)
        terms = (g_gain1, g_bias1, g_qkv, g_qv, g_out, g_obias, g_gain2, g_bias2, g_up, g_ubias, g_down, g_dbias)
        carry = tuple((total + term for total, term in zip(carry, terms)))
        return (carry, (output, grad_inputs))
    start = (jnp.zeros((model,), f32), jnp.zeros((model,), f32), jnp.zeros((model, 3 * model), f32), jnp.zeros((2 * model,), f32), jnp.zeros((model, model), f32), jnp.zeros((model,), f32), jnp.zeros((model,), f32), jnp.zeros((model,), f32), jnp.zeros((model, FF), f32), jnp.zeros((FF,), f32), jnp.zeros((FF, model), f32), jnp.zeros((model,), f32))
    totals, stacked = lax.scan(one_sequence, start, (tokens, cotangent, positions))
    return (stacked[0], stacked[1], totals[0], totals[1], totals[2], totals[3], totals[4], totals[5], totals[6], totals[7], totals[8], totals[9], totals[10], totals[11])
```

```python
import math

import jax
import jax.numpy as jnp
from jax import lax
from jax.sharding import PartitionSpec as P

HEAD = 64


EPS = 1e-05
GELU_C = 0.7978845608028654


def gelu_value(hidden):
    return 0.5 * hidden * (1.0 + jnp.tanh(GELU_C * (hidden + 0.044715 * hidden * hidden * hidden)))


def gelu_slope(hidden):
    inner = jnp.tanh(GELU_C * (hidden + 0.044715 * hidden * hidden * hidden))
    return 0.5 * (1.0 + inner) + 0.5 * hidden * (1.0 - inner * inner) * GELU_C * (
        1.0 + 3.0 * 0.044715 * hidden * hidden
    )


def norm_apply(values):
    centred = values - jnp.mean(values, -1, keepdims=True)
    inv_std = lax.rsqrt(jnp.mean(centred * centred, -1, keepdims=True) + EPS)
    return (centred * inv_std, inv_std)


def norm_back(grad_norm, normed, inv_std):
    return inv_std * (
        grad_norm
        - jnp.mean(grad_norm, -1, keepdims=True)
        - normed * jnp.mean(grad_norm * normed, -1, keepdims=True)
    )


def masked_scores(query_h, keys_h, allowed, scale_qk):
    scores = (
        jnp.einsum("qhd,khd->hqk", query_h, keys_h, preferred_element_type=jnp.float32) * scale_qk
    )
    return jnp.where(allowed[None], scores, -jnp.inf)


def gathered_plan(
    tokens,
    cotangent,
    positions,
    ln1_gain,
    ln1_bias,
    w_qkv,
    qv_bias,
    w_out,
    out_bias,
    ln2_gain,
    ln2_bias,
    w_up,
    up_bias,
    w_down,
    down_bias,
):
    f32 = jnp.float32
    bf16 = jnp.bfloat16
    slots = tokens.shape[1]
    model = tokens.shape[2]
    groups = lax.axis_size("grp")
    length = slots * groups
    heads = model // HEAD
    scale_qk = 1.0 / math.sqrt(HEAD)
    here = lax.axis_index("grp")
    key_pos = positions[0]
    query_pos = lax.dynamic_slice_in_dim(key_pos, here * slots, slots)
    allowed = key_pos[None, :] <= query_pos[:, None]
    gain1, bias1, full_qkv, full_qv, full_out, full_obias = (
        lax.all_gather(ln1_gain, "grp", axis=0, tiled=True),
        lax.all_gather(ln1_bias, "grp", axis=0, tiled=True),
        lax.all_gather(w_qkv, "grp", axis=0, tiled=True),
        lax.all_gather(qv_bias, "grp", axis=0, tiled=True),
        lax.all_gather(w_out, "grp", axis=0, tiled=True),
        lax.all_gather(out_bias, "grp", axis=0, tiled=True),
    )
    inputs = tokens[0].astype(f32)
    normed1, inv1 = norm_apply(inputs)
    act1 = (normed1 * gain1.astype(f32) + bias1.astype(f32)).astype(bf16)
    proj = jnp.dot(act1, full_qkv, preferred_element_type=f32)
    qv_float = full_qv.astype(f32)
    query = (proj[:, :model] + qv_float[:model]).astype(bf16)
    keys_local = proj[:, model : 2 * model].astype(bf16)
    values_local = (proj[:, 2 * model :] + qv_float[model:]).astype(bf16)
    keys_all, values_all = (
        lax.all_gather(keys_local, "grp", axis=0, tiled=True),
        lax.all_gather(values_local, "grp", axis=0, tiled=True),
    )
    query_h = query.reshape(slots, heads, HEAD)
    keys_h = keys_all.reshape(length, heads, HEAD)
    values_h = values_all.reshape(length, heads, HEAD)
    scores = masked_scores(query_h, keys_h, allowed, scale_qk)
    peak = jnp.max(scores, -1, keepdims=True)
    log_total = peak + jnp.log(jnp.sum(jnp.exp(scores - peak), -1, keepdims=True))
    probs_b = jnp.exp(scores - log_total).astype(bf16)
    attended = (
        jnp.einsum("hqk,khd->qhd", probs_b, values_h, preferred_element_type=f32)
        .reshape(slots, model)
        .astype(bf16)
    )
    middle = (
        inputs + jnp.dot(attended, full_out, preferred_element_type=f32) + full_obias.astype(f32)
    )
    gain2, bias2, full_up, full_ubias, full_down, full_dbias = (
        lax.all_gather(ln2_gain, "grp", axis=0, tiled=True),
        lax.all_gather(ln2_bias, "grp", axis=0, tiled=True),
        lax.all_gather(w_up, "grp", axis=0, tiled=True),
        lax.all_gather(up_bias, "grp", axis=0, tiled=True),
        lax.all_gather(w_down, "grp", axis=0, tiled=True),
        lax.all_gather(down_bias, "grp", axis=0, tiled=True),
    )
    normed2, inv2 = norm_apply(middle)
    act2 = (normed2 * gain2.astype(f32) + bias2.astype(f32)).astype(bf16)
    hidden = jnp.dot(act2, full_up, preferred_element_type=f32) + full_ubias.astype(f32)
    activ = gelu_value(hidden).astype(bf16)
    output = middle + jnp.dot(activ, full_down, preferred_element_type=f32) + full_dbias.astype(f32)
    grad_out = cotangent[0]
    grad_float = grad_out.astype(f32)
    grad_act = jnp.dot(grad_out, full_down.T, preferred_element_type=f32)
    grad_hidden = (grad_act * gelu_slope(hidden)).astype(bf16)
    grad_norm2 = jnp.dot(grad_hidden, full_up.T, preferred_element_type=f32)
    g_gain2 = jnp.sum(grad_norm2 * normed2, 0)
    g_bias2 = jnp.sum(grad_norm2, 0)
    grad_middle = grad_float + norm_back(grad_norm2 * gain2.astype(f32), normed2, inv2)
    hidden_units = hidden.shape[1]
    d_share = model // groups
    gh_all, gout_all = (
        lax.all_gather(grad_hidden, "grp", axis=0, tiled=True),
        lax.all_gather(grad_out, "grp", axis=0, tiled=True),
    )
    own_act, own_activ = (
        lax.all_to_all(act2, "grp", split_axis=1, concat_axis=0, tiled=True),
        lax.all_to_all(activ, "grp", split_axis=1, concat_axis=0, tiled=True),
    )
    f_share = hidden_units // groups
    g_up = jnp.dot(own_act.T, gh_all, preferred_element_type=f32)
    own_gh = lax.dynamic_slice_in_dim(gh_all, here * f_share, f_share, 1)
    g_ubias = jnp.sum(own_gh.astype(f32), 0)
    g_down = jnp.dot(own_activ.T, gout_all, preferred_element_type=f32)
    own_gout = lax.dynamic_slice_in_dim(gout_all, here * d_share, d_share, 1)
    g_dbias = jnp.sum(own_gout.astype(f32), 0)
    grad_mid_b = grad_middle.astype(bf16)
    g_obias = jnp.sum(grad_middle, 0)
    grad_att = jnp.dot(grad_mid_b, full_out.T, preferred_element_type=f32).astype(bf16)
    grad_att_h = grad_att.reshape(slots, heads, HEAD)
    attended_h = attended.reshape(slots, heads, HEAD)
    probs_again = jnp.exp(masked_scores(query_h, keys_h, allowed, scale_qk) - log_total)
    probs_again_b = probs_again.astype(bf16)
    grad_probs = jnp.einsum("qhd,khd->hqk", grad_att_h, values_h, preferred_element_type=f32)
    delta = jnp.einsum("qhd,qhd->hq", grad_att_h, attended_h, preferred_element_type=f32)[..., None]
    grad_scores = (probs_again * (grad_probs - delta) * scale_qk).astype(bf16)
    grad_query = jnp.einsum(
        "hqk,khd->qhd", grad_scores, keys_h, preferred_element_type=f32
    ).reshape(slots, model)
    grad_keys_all = jnp.einsum(
        "hqk,qhd->khd", grad_scores, query_h, preferred_element_type=f32
    ).reshape(length, model)
    grad_values_all = jnp.einsum(
        "hqk,qhd->khd", probs_again_b, grad_att_h, preferred_element_type=f32
    ).reshape(length, model)
    grad_keys, grad_values = (
        lax.psum_scatter(grad_keys_all, "grp", scatter_dimension=0, tiled=True),
        lax.psum_scatter(grad_values_all, "grp", scatter_dimension=0, tiled=True),
    )
    grad_proj = jnp.concatenate([grad_query, grad_keys, grad_values], 1).astype(bf16)
    grad_norm1 = jnp.dot(grad_proj, full_qkv.T, preferred_element_type=f32)
    g_gain1 = jnp.sum(grad_norm1 * normed1, 0)
    g_bias1 = jnp.sum(grad_norm1, 0)
    grad_inputs = grad_middle + norm_back(grad_norm1 * gain1.astype(f32), normed1, inv1)
    proj_all, mid_all = (
        lax.all_gather(grad_proj, "grp", axis=0, tiled=True),
        lax.all_gather(grad_mid_b, "grp", axis=0, tiled=True),
    )
    own_act1, own_attended = (
        lax.all_to_all(act1, "grp", split_axis=1, concat_axis=0, tiled=True),
        lax.all_to_all(attended, "grp", split_axis=1, concat_axis=0, tiled=True),
    )
    s_qkv = jnp.dot(own_act1.T, proj_all, preferred_element_type=f32)
    s_out = jnp.dot(own_attended.T, mid_all, preferred_element_type=f32)
    qv_whole = jnp.concatenate(
        [
            jnp.sum(proj_all[:, :model].astype(f32), 0),
            jnp.sum(proj_all[:, 2 * model :].astype(f32), 0),
        ]
    )
    qv_share = 2 * d_share
    s_qv = lax.dynamic_slice_in_dim(qv_whole, here * qv_share, qv_share)
    s_gain1, s_bias1, s_obias, s_gain2, s_bias2 = (
        lax.psum_scatter(g_gain1, "grp", scatter_dimension=0, tiled=True),
        lax.psum_scatter(g_bias1, "grp", scatter_dimension=0, tiled=True),
        lax.psum_scatter(g_obias, "grp", scatter_dimension=0, tiled=True),
        lax.psum_scatter(g_gain2, "grp", scatter_dimension=0, tiled=True),
        lax.psum_scatter(g_bias2, "grp", scatter_dimension=0, tiled=True),
    )
    summed = lax.psum(
        (
            s_gain1,
            s_bias1,
            s_qkv,
            s_qv,
            s_out,
            s_obias,
            s_gain2,
            s_bias2,
            g_up,
            g_ubias,
            g_down,
            g_dbias,
        ),
        "rep",
    )
    return (
        output[None],
        grad_inputs[None],
        summed[0],
        summed[1],
        summed[2],
        summed[3],
        summed[4],
        summed[5],
        summed[6],
        summed[7],
        summed[8],
        summed[9],
        summed[10],
        summed[11],
    )


GRP_SWAP = [(0, 1), (1, 0)]
COPY_ROWS = 8


def fast_plan(
    tokens,
    cotangent,
    positions,
    ln1_gain,
    ln1_bias,
    w_qkv,
    qv_bias,
    w_out,
    out_bias,
    ln2_gain,
    ln2_bias,
    w_up,
    up_bias,
    w_down,
    down_bias,
):
    f32 = jnp.float32
    bf16 = jnp.bfloat16
    slots = tokens.shape[1]
    model = tokens.shape[2]
    heads = model // HEAD
    scale_qk = 1.0 / math.sqrt(HEAD)
    reps = lax.axis_size("rep")
    rep = lax.axis_index("rep")
    grp = lax.axis_index("grp")
    core = rep % 2
    row_y = (rep // 2) % 2
    part = (rep // 2) % 4
    pos_z = rep // 4
    zs = reps // 4

    def flip(array, bit):
        return lax.ppermute(array, "rep", [(i, i ^ bit) for i in range(reps)])

    def over_core(array):
        return flip(array, 1)

    def over_y(array):
        return flip(array, 2)

    def over_z(array):
        return flip(array, 4)

    def over_x(array):
        return lax.ppermute(array, "grp", GRP_SWAP)

    home = core == grp
    turn = [
        (2 * r + g, 2 * (r - r % 2 + g) + r % 2)
        for r in range(reps)
        for g in range(2)
        if r % 2 != g
    ]

    def regroup(array):
        moved = lax.ppermute(array, ("rep", "grp"), turn)
        return jnp.where(home, array, moved)

    def fetch_half(weight, direct):
        rows, columns = weight.shape
        tiles = rows // COPY_ROWS
        quarter = tiles // 4
        take = (quarter + 1) // 2
        tiled = weight.reshape(tiles, COPY_ROWS, columns)

        def start(which, side):
            return which * quarter + side * (quarter - take)

        def cut(which):
            return lax.dynamic_slice_in_dim(tiled, start(which, core), take, 0)

        mine = over_x(cut(part))
        across = over_x(cut(part ^ 3)) if direct else None
        by_y = over_y(mine)
        by_z = over_z(mine)
        pieces = [(mine, part, 0), (by_y, part ^ 1, 0), (by_z, part ^ 2, 0)]
        if direct:
            pieces.append((across, part ^ 3, 0))
        else:
            some = take // 2
            pieces.append((over_y(by_z[:some]), part ^ 3, 0))
            pieces.append((over_z(by_y[some:]), part ^ 3, some))
        whole = jnp.concatenate([tiled, tiled], 0)
        base = (1 - grp) * tiles
        for piece, which, skip in pieces:
            at = base + start(which, core) + skip
            whole = lax.dynamic_update_slice_in_dim(whole, piece, at, 0)
        for piece, which, skip in pieces:
            at = base + start(which, 1 - core) + skip
            whole = lax.dynamic_update_slice_in_dim(whole, over_core(piece), at, 0)
        return whole.reshape(2 * rows, columns)

    def pick(array, index, size):
        return lax.dynamic_slice_in_dim(array, index * size, size, array.ndim - 1)

    def spread_rows(array):
        pair = jnp.concatenate([array, over_x(array)], 0)
        return jnp.concatenate([pair, over_core(pair)], 0)

    def spread_columns(array):
        half = array.shape[1] // 2
        pair = jnp.concatenate(
            [pick(array, grp, half), over_x(pick(array, 1 - grp, half))], 0
        )
        quarter = half // 2
        return jnp.concatenate(
            [pick(pair, core, quarter), over_core(pick(pair, 1 - core, quarter))], 0
        )

    inner_z = jnp.logical_and(pos_z > 0, pos_z < zs - 1)
    inward = [(i, i + 4) for i in range(4)] + [(i, i - 4) for i in range(12, 16)]
    middle_z = [(i, i + 4) for i in range(4, 8)] + [(i, i - 4) for i in range(8, 12)]
    outward = [(b, a) for a, b in inward]

    def reduce_rows(total):
        rows, columns = total.shape
        own_rows = rows // 2
        split = total.reshape(2, own_rows, columns)
        away = lax.dynamic_index_in_dim(split, 1 - row_y, 0, False).astype(bf16)
        near = lax.dynamic_index_in_dim(split, row_y, 0, False)
        part_sum = near + over_y(away).astype(f32)
        line = part_sum + lax.ppermute(part_sum.astype(bf16), "rep", inward).astype(f32)
        line_b = line.astype(bf16)
        met = lax.ppermute(line_b, "rep", middle_z)
        full = (line_b.astype(f32) + met.astype(f32)).astype(bf16)
        done = jnp.where(inner_z, full, lax.ppermute(full, "rep", outward))
        other = over_y(done)
        out = jnp.zeros((4, own_rows, columns), f32)
        for piece, index in (
            (done, 2 * core + row_y),
            (other, 2 * core + 1 - row_y),
            (over_core(done), 2 * (1 - core) + row_y),
            (over_core(other), 2 * (1 - core) + 1 - row_y),
        ):
            out = lax.dynamic_update_index_in_dim(out, piece.astype(f32), index, 0)
        return out.reshape(2 * rows, columns)

    small = (ln1_gain, ln1_bias, qv_bias, out_bias, ln2_gain, ln2_bias, up_bias, down_bias)
    packed = jnp.concatenate([one.reshape(1, -1) for one in small], 1)
    packed_far = over_x(packed)
    both = jnp.where(
        grp == 0,
        jnp.concatenate([packed, packed_far], 0),
        jnp.concatenate([packed_far, packed], 0),
    ).astype(f32)
    wholes = []
    at = 0
    for one in small:
        wholes.append(both[:, at : at + one.shape[0]].reshape(-1))
        at += one.shape[0]
    gain1, bias1, qv_float, obias, gain2, bias2, ubias, dbias = wholes

    seq_tokens = regroup(tokens[0])
    seq_pos = regroup(positions[0])
    full_qkv = fetch_half(w_qkv, True)
    grad_out = regroup(cotangent[0])
    full_out = fetch_half(w_out, False)
    full_up = fetch_half(w_up, False)
    full_down = fetch_half(w_down, False)

    query_pos = lax.dynamic_slice_in_dim(seq_pos, core * slots, slots)
    far_pos = lax.dynamic_slice_in_dim(seq_pos, (1 - core) * slots, slots)
    key_pos = jnp.concatenate([query_pos, far_pos])
    allowed = key_pos[None, :] <= query_pos[:, None]

    inputs = seq_tokens.astype(f32)
    normed1, inv1 = norm_apply(inputs)
    act1 = (normed1 * gain1 + bias1).astype(bf16)
    proj = jnp.dot(act1, full_qkv, preferred_element_type=f32)
    query = (proj[:, :model] + qv_float[:model]).astype(bf16)
    keys_local = proj[:, model : 2 * model].astype(bf16)
    values_local = (proj[:, 2 * model :] + qv_float[model:]).astype(bf16)
    keys_all = jnp.concatenate([keys_local, over_core(keys_local)], 0)
    values_all = jnp.concatenate([values_local, over_core(values_local)], 0)
    length = 2 * slots
    query_h = query.reshape(slots, heads, HEAD)
    keys_h = keys_all.reshape(length, heads, HEAD)
    values_h = values_all.reshape(length, heads, HEAD)
    scores = masked_scores(query_h, keys_h, allowed, scale_qk)
    peak = jnp.max(scores, -1, keepdims=True)
    log_total = peak + jnp.log(jnp.sum(jnp.exp(scores - peak), -1, keepdims=True))
    probs = jnp.exp(scores - log_total)
    probs_b = probs.astype(bf16)
    attended = (
        jnp.einsum("hqk,khd->qhd", probs_b, values_h, preferred_element_type=f32)
        .reshape(slots, model)
        .astype(bf16)
    )
    middle = inputs + jnp.dot(attended, full_out, preferred_element_type=f32) + obias
    normed2, inv2 = norm_apply(middle)
    act2 = (normed2 * gain2 + bias2).astype(bf16)
    hidden = jnp.dot(act2, full_up, preferred_element_type=f32) + ubias
    activ = gelu_value(hidden).astype(bf16)
    grad_float = grad_out.astype(f32)

    gout_all = spread_rows(grad_out)
    g_down = reduce_rows(
        jnp.dot(spread_columns(activ).T, gout_all, preferred_element_type=f32)
    )
    grad_act = jnp.dot(grad_out, full_down.T, preferred_element_type=f32)
    grad_hidden = (grad_act * gelu_slope(hidden)).astype(bf16)
    g_up = reduce_rows(
        jnp.dot(spread_columns(act2).T, spread_rows(grad_hidden), preferred_element_type=f32)
    )
    output = middle + jnp.dot(activ, full_down, preferred_element_type=f32) + dbias
    output = regroup(output)

    grad_norm2 = jnp.dot(grad_hidden, full_up.T, preferred_element_type=f32)
    g_gain2 = jnp.sum(grad_norm2 * normed2, 0)
    g_bias2 = jnp.sum(grad_norm2, 0)
    grad_middle = grad_float + norm_back(grad_norm2 * gain2, normed2, inv2)
    grad_mid_b = grad_middle.astype(bf16)
    g_obias = jnp.sum(grad_middle, 0)
    s_out = reduce_rows(
        jnp.dot(
            spread_columns(attended).T, spread_rows(grad_mid_b), preferred_element_type=f32
        )
    )
    grad_att = jnp.dot(grad_mid_b, full_out.T, preferred_element_type=f32).astype(bf16)
    grad_att_h = grad_att.reshape(slots, heads, HEAD)
    attended_h = attended.reshape(slots, heads, HEAD)
    grad_probs = jnp.einsum("qhd,khd->hqk", grad_att_h, values_h, preferred_element_type=f32)
    delta = jnp.einsum("qhd,qhd->hq", grad_att_h, attended_h, preferred_element_type=f32)[..., None]
    grad_scores = (probs * (grad_probs - delta) * scale_qk).astype(bf16)
    grad_query = jnp.einsum(
        "hqk,khd->qhd", grad_scores, keys_h, preferred_element_type=f32
    ).reshape(slots, model)
    grad_keys_all = jnp.einsum(
        "hqk,qhd->khd", grad_scores, query_h, preferred_element_type=f32
    ).reshape(length, model)
    grad_values_all = jnp.einsum(
        "hqk,qhd->khd", probs_b, grad_att_h, preferred_element_type=f32
    ).reshape(length, model)
    grad_keys = grad_keys_all[:slots] + over_core(grad_keys_all[slots:])
    grad_values = grad_values_all[:slots] + over_core(grad_values_all[slots:])
    grad_proj = jnp.concatenate([grad_query, grad_keys, grad_values], 1).astype(bf16)
    s_qkv = reduce_rows(
        jnp.dot(spread_columns(act1).T, spread_rows(grad_proj), preferred_element_type=f32)
    )
    grad_norm1 = jnp.dot(grad_proj, full_qkv.T, preferred_element_type=f32)
    g_gain1 = jnp.sum(grad_norm1 * normed1, 0)
    g_bias1 = jnp.sum(grad_norm1, 0)
    grad_inputs = grad_middle + norm_back(grad_norm1 * gain1, normed1, inv1)
    grad_inputs = regroup(grad_inputs)

    proj_float = grad_proj.astype(f32)
    g_qv = jnp.concatenate(
        [jnp.sum(proj_float[:, :model], 0), jnp.sum(proj_float[:, 2 * model :], 0)]
    )
    g_ubias = jnp.sum(grad_hidden.astype(f32), 0)
    g_dbias = jnp.sum(grad_float, 0)
    vectors = (g_gain1, g_bias1, g_qv, g_obias, g_gain2, g_bias2, g_ubias, g_dbias)
    rows = jnp.concatenate([one.reshape(2, -1) for one in vectors], 1)
    line = lax.dynamic_slice_in_dim(rows, grp, 1, 0) + over_x(
        lax.dynamic_slice_in_dim(rows, 1 - grp, 1, 0)
    )
    bit = 1
    while bit < reps:
        line = line + flip(line, bit)
        bit *= 2
    sums = []
    at = 0
    for one in vectors:
        width = one.shape[0] // 2
        sums.append(line[0, at : at + width])
        at += width
    s_gain1, s_bias1, s_qv, s_obias, s_gain2, s_bias2, g_ubias, g_dbias = sums
    return (
        output[None],
        grad_inputs[None],
        s_gain1,
        s_bias1,
        s_qkv,
        s_qv,
        s_out,
        s_obias,
        s_gain2,
        s_bias2,
        g_up,
        g_ubias,
        g_down,
        g_dbias,
    )


def solution(mesh):
    paired = mesh.shape["grp"] == 2 and mesh.shape["rep"] == 16
    return jax.shard_map(
        fast_plan if paired else gathered_plan,
        mesh=mesh,
        in_specs=(
            P("rep", "grp", None),
            P("rep", "grp", None),
            P("rep", None),
            P("grp"),
            P("grp"),
            P("grp", None),
            P("grp"),
            P("grp", None),
            P("grp"),
            P("grp"),
            P("grp"),
            P("grp", None),
            P("grp"),
            P("grp", None),
            P("grp"),
        ),
        out_specs=(
            P("rep", "grp", None),
            P("rep", "grp", None),
            P("grp"),
            P("grp"),
            P("grp", None),
            P("grp"),
            P("grp", None),
            P("grp"),
            P("grp"),
            P("grp"),
            P("grp", None),
            P("grp"),
            P("grp", None),
            P("grp"),
        ),
        check_vma=False,
    )
```
